32 devices in a mesh: ctx: 8 (over y, x, core), tp: 4 (over z).
Axes of the slice: x: 2, y: 2, z: 4, core: 2. Of those that a mesh axis runs over, the one named last changes fastest.
Arguments:
- activations: bfloat16 [2048, 4096], P(('ctx', 'tp')), may hold values from -6 to 6
- input_proj: bfloat16 [4096, 3, 2048], P(None, None, 'tp'), may hold values from -0.09375 to 0.09375
- short_taps: float32 [3, 7, 2048], P(None, None, 'tp'), may hold values from -2 to 2
- medium_taps: float32 [128, 128], P('tp'), may hold values from -0.5 to 0.5
- skip_gain: float32 [2048], P('tp'), may hold values from -4 to 4
- output_proj: bfloat16 [2048, 4096], P('tp'), may hold values from -0.125 to 0.125
- out_grad: bfloat16 [2048, 4096], P(('ctx', 'tp')), may hold values from -6 to 6
Outputs:
- layer_out: bfloat16 [2048, 4096], P(('ctx', 'tp'))
- act_grad: bfloat16 [2048, 4096], P(('ctx', 'tp'))
The draws below stay inside these ranges and needn't reach their ends.
All inputs are finite; a program needn't handle non-finite values.
Results may differ from the reference program's by a relative error of at most 0.015.
Values may be sent and summed in bfloat16 or wider, within the bound.
A program may use at most 128 MiB of HBM per device.

```python
import jax
import jax.numpy as jnp
from jax import lax

D = 4096
CH = 2048
SHORT = 7
MED = 128
GROUP_SIZE = 16
GROUPS = 128
TOKENS = 2048
N_TP = 4


def levels(stream_key, extent, split, smallest, top_value):
    level = 1.0
    for position, shards_of in split:
        heights = jax.random.uniform(jax.random.fold_in(jax.random.fold_in(stream_key, 6), position), (shards_of,), jnp.float32, smallest / len(split), top_value / len(split))
        level = level * jnp.repeat(jnp.exp(heights), extent[position] // shards_of).reshape((-1,) + (1,) * (len(extent) - 1 - position))
    return level


def noise(stream_key, shape, width, bound, shards=(), held_as=jnp.bfloat16):
    array = jax.random.normal(stream_key, shape, jnp.float32) * width
    if len(shards) > 0:
        array = levels(stream_key, shape, shards, -0.22, 0.18) * array
    return jnp.clip(array, min=-bound, max=bound).astype(held_as)


def setup_inputs(seed: int = 0) -> dict:
    streams_of = jax.random.split(jax.random.key(seed), 8)
    activations = noise(streams_of[0], (TOKENS, D), 1.0, 6.0, ((0, 32),))
    input_proj = noise(streams_of[1], (D, 3, CH), D ** -0.5, 0.09375, ((2, 4),))
    short_taps = noise(streams_of[2], (3, SHORT, CH), SHORT ** -0.5, 2.0, ((2, 4),), jnp.float32)
    medium_taps = noise(streams_of[3], (GROUPS, MED), MED ** -0.5, 0.5, ((0, 4),), jnp.float32)
    skip_gain = noise(streams_of[4], (CH,), 1.0, 4.0, ((0, 4),), jnp.float32)
    output_proj = noise(streams_of[5], (CH, D), CH ** -0.5, 0.125, ((0, 4),))
    out_grad = noise(streams_of[6], (TOKENS, D), 1.0, 6.0, ((0, 32),))
    return {"activations": activations, "input_proj": input_proj, "short_taps": short_taps, "medium_taps": medium_taps, "skip_gain": skip_gain, "output_proj": output_proj, "out_grad": out_grad}


def rounded(value):
    return lax.optimization_barrier(value.astype(jnp.bfloat16)).astype(jnp.float32)


def reference(activations, input_proj, short_taps, medium_taps, skip_gain, output_proj, out_grad):
    block = CH // N_TP
    contract = (((1,), (1,)), ((), ()))
    lead = SHORT - 1
    projected = jnp.dot(activations, input_proj.reshape(D, 3 * CH), preferred_element_type=jnp.float32)
    projected = projected.astype(jnp.bfloat16).reshape(TOKENS, 3, CH)
    padded = jnp.concatenate([jnp.zeros((lead, 3, CH), jnp.bfloat16), projected], axis=0)
    total = jnp.zeros((TOKENS, 3, CH), jnp.float32)
    for lag in range(SHORT):
        total = total + short_taps[:, lag, :] * padded[lead - lag: lead - lag + TOKENS].astype(jnp.float32)
    filtered = total.astype(jnp.bfloat16)
    query = filtered[:, 0].astype(jnp.float32)
    keyed = filtered[:, 1].astype(jnp.float32)
    valued = filtered[:, 2].astype(jnp.float32)
    mixed = keyed * valued
    filters = jnp.repeat(medium_taps, GROUP_SIZE, axis=0).T
    mixed_pad = jnp.concatenate([jnp.zeros((MED - 1, CH), jnp.float32), mixed], axis=0)

    def causal_step(lag, acc):
        piece = lax.dynamic_slice_in_dim(mixed_pad, (MED - 1 - lag).astype(jnp.int32), TOKENS, 0)
        return acc + filters[lag] * piece

    inner = lax.fori_loop(0, MED, causal_step, skip_gain * mixed)
    gated = (query * inner).astype(jnp.bfloat16)
    out_total = jnp.zeros((TOKENS, D), jnp.float32)
    for index in range(N_TP):
        low = index * block
        out_total = out_total + rounded(jnp.dot(gated[:, low:low + block], output_proj[low:low + block], preferred_element_type=jnp.float32))
    layer_out = out_total.astype(jnp.bfloat16)

    grad_gated = lax.dot_general(out_grad, output_proj, contract, preferred_element_type=jnp.float32)
    grad_query = (grad_gated * inner).astype(jnp.bfloat16)
    grad_inner = (grad_gated * query).astype(jnp.bfloat16)
    inner_pad = jnp.concatenate([grad_inner.astype(jnp.float32), jnp.zeros((MED - 1, CH), jnp.float32)], axis=0)

    def anti_step(lag, acc):
        piece = lax.dynamic_slice_in_dim(inner_pad, lag.astype(jnp.int32), TOKENS, 0)
        return acc + filters[lag] * piece

    grad_mixed = lax.fori_loop(0, MED, anti_step, skip_gain * grad_inner.astype(jnp.float32))
    grad_filtered = jnp.stack([grad_query.astype(jnp.float32), grad_mixed * valued, grad_mixed * keyed], axis=1)
    grad_pad = jnp.concatenate([grad_filtered, jnp.zeros((lead, 3, CH), jnp.float32)], axis=0)
    total = jnp.zeros((TOKENS, 3, CH), jnp.float32)
    for lag in range(SHORT):
        total = total + short_taps[:, lag, :] * grad_pad[lag: lag + TOKENS]
    grad_projected = total.astype(jnp.bfloat16)
    grad_total = jnp.zeros((TOKENS, D), jnp.float32)
    for index in range(N_TP):
        low = index * block
        left = grad_projected[:, :, low:low + block].reshape(TOKENS, 3 * block)
        right = input_proj[:, :, low:low + block].reshape(D, 3 * block)
        grad_total = grad_total + rounded(lax.dot_general(left, right, contract, preferred_element_type=jnp.float32))
    act_grad = grad_total.astype(jnp.bfloat16)
    return (layer_out, act_grad)
```

```python
import functools

import jax
import jax.numpy as jnp
from jax import lax
from jax.experimental import pallas as pl
from jax.experimental.pallas import tpu as pltpu
from jax.sharding import PartitionSpec as P

GROUP_SIZE = 16
LANES = 128
MESH = pl.DeviceIdType.MESH
F32 = jnp.float32
BF16 = jnp.bfloat16
NT = (((1,), (1,)), ((), ()))


def kernel(
    n, blocks, halo, lead,
    act_hbm, w_hbm, short_ref, med_ref, skip_ref, o_hbm, grad_hbm,
    out_ref, dact_ref,
    w, o, acts, grads, taps, pext, bext, gext, query, inner, gated, ggate, gproj, shifted,
    rs1, rs1_l, rs1_r, rs2, rs2_l, rs2_r,
    local_sem, bar_send, halo_send, halo_recv, *sems,
):
    me = lax.axis_index("tp")
    blk = lax.axis_index("ctx")
    rows, width = act_hbm.shape
    channels = w_hbm.shape[2]
    total = rows * n
    span = med_ref.shape[1]
    shorts = short_ref.shape[1]
    tiles = channels // LANES
    right = {"ctx": blk, "tp": me + 1}
    left = {"ctx": blk, "tp": me - 1}
    has_right = me + 1 < n
    has_left = me > 0
    has_next = blk + 1 < blocks
    has_prev = blk > 0

    def to(src, dst, send, recv, where):
        return pltpu.make_async_remote_copy(
            src_ref=src, dst_ref=dst, send_sem=send, recv_sem=recv,
            device_id=where, device_id_type=MESH,
        )

    loads = [
        pltpu.make_async_copy(act_hbm, acts.at[me], local_sem.at[0]),
        pltpu.make_async_copy(w_hbm, w, local_sem.at[1]),
        pltpu.make_async_copy(grad_hbm, grads.at[me], local_sem.at[2]),
        pltpu.make_async_copy(o_hbm, o, local_sem.at[3]),
    ]
    for load in loads:
        load.start()

    barrier = pltpu.get_barrier_semaphore()
    nbr = [
        (has_right, right), (has_left, left),
        (has_next, {"ctx": blk + 1, "tp": me}), (has_prev, {"ctx": blk - 1, "tp": me}),
    ]
    for cond, where in nbr:
        @pl.when(cond)
        def _(where=where):
            pl.semaphore_signal(barrier, inc=1, device_id=where, device_id_type=MESH)
    peers = sum(jnp.where(cond, 1, 0) for cond, _ in nbr)
    pl.semaphore_wait(barrier, peers)

    ga = sems[0:4]
    gg = sems[4:8]

    def send_right(buf, own, s, shard, first):
        src = own if first else buf.at[shard]
        to(src, buf.at[shard], s[0].at[shard], s[1].at[shard], right).start()

    def send_left(buf, own, s, shard, first):
        src = own if first else buf.at[shard]
        to(src, buf.at[shard], s[2].at[shard], s[3].at[shard], left).start()

    def from_left(buf, s, shard):
        to(buf.at[shard], buf.at[shard], s[0].at[shard], s[1].at[shard], left).wait_recv()

    def from_right(buf, s, shard):
        to(buf.at[shard], buf.at[shard], s[2].at[shard], s[3].at[shard], right).wait_recv()

    def gather_drain(buf, s):
        def one(i, carry):
            @pl.when(has_right & (i <= me))
            def _():
                to(buf.at[i], buf.at[i], s[0].at[i], s[1].at[i], right).wait_send()

            @pl.when(has_left & (i >= me))
            def _():
                to(buf.at[i], buf.at[i], s[2].at[i], s[3].at[i], left).wait_send()

            return carry

        lax.fori_loop(0, n, one, 0)

    def grad_own(step):
        @pl.when(has_right & (me == step))
        def _():
            send_right(grads, grad_hbm, gg, me, True)

        @pl.when(has_left & (n - 1 - me == step))
        def _():
            send_left(grads, grad_hbm, gg, me, True)

    @pl.when(has_right)
    def _():
        send_right(acts, act_hbm, ga, me, True)

    @pl.when(has_left)
    def _():
        send_left(acts, act_hbm, ga, me, True)

    grad_own(0)

    groups = med_ref.shape[0]
    ig = lax.broadcasted_iota(jnp.int32, (groups, channels), 0) * GROUP_SIZE
    ic = lax.broadcasted_iota(jnp.int32, (groups, channels), 1)
    spread = jnp.where((ic >= ig) & (ic < ig + GROUP_SIZE), 1.0, 0.0).astype(F32)
    taps[...] = lax.dot_general(
        med_ref[...], spread, (((0,), (0,)), ((), ())),
        precision=lax.Precision.HIGHEST, preferred_element_type=F32,
    )
    taps[0:1, :] = taps[0:1, :] + skip_ref[...]

    def project(shard):
        x = acts[shard]
        at = pl.ds(pl.multiple_of(halo + shard * rows, 16), rows)
        for s in range(3):
            pext[s, at, :] = jnp.dot(x, w[s], preferred_element_type=F32).astype(BF16)

    def grad_gate(shard):
        at = pl.ds(pl.multiple_of(shard * rows, 16), rows)
        ggate[at, :] = lax.dot_general(grads[shard], o[...], NT, preferred_element_type=F32)

    def step(buf, s, k, use):
        l, r = me - k, me + k

        @pl.when(l >= 0)
        def _():
            from_left(buf, s, l)

            @pl.when(has_right)
            def _():
                send_right(buf, None, s, l, False)

        @pl.when(r < n)
        def _():
            from_right(buf, s, r)

            @pl.when(has_left)
            def _():
                send_left(buf, None, s, r, False)

        if use is project:
            grad_own(k)

        @pl.when(l >= 0)
        def _():
            use(l)

        @pl.when(r < n)
        def _():
            use(r)

    loads[0].wait()
    loads[1].wait()
    project(me)

    def act_step(k, carry):
        step(acts, ga, k, project)
        return carry

    lax.fori_loop(1, n, act_step, 0)

    def fwd_halo():
        return to(
            pext.at[:, pl.ds(total, halo), :], pext.at[:, pl.ds(0, halo), :],
            halo_send.at[0], halo_recv.at[0], {"ctx": blk + 1, "tp": me},
        )

    def fwd_halo_in():
        return to(
            pext.at[:, pl.ds(total, halo), :], pext.at[:, pl.ds(0, halo), :],
            halo_send.at[0], halo_recv.at[0], {"ctx": blk - 1, "tp": me},
        )

    @pl.when(has_next)
    def _():
        fwd_halo().start()

    loads[2].wait()
    loads[3].wait()
    grad_gate(me)

    @pl.when(has_prev)
    def _():
        fwd_halo_in().wait_recv()

    @pl.when(jnp.logical_not(has_prev))
    def _():
        pext[:, 0:halo, :] = jnp.zeros((3, halo, channels), BF16)

    def lane(l):
        return pl.ds(pl.multiple_of(l * LANES, LANES), LANES)

    def correlate(lanes, count, base, sign):
        def tap_rows(q, acc):
            block = taps[pl.ds(pl.multiple_of(8 * q, 8), 8), lanes]
            start = pl.multiple_of(base + sign * 8 * q, 8)
            for r in range(8):
                acc = acc + block[r : r + 1] * shifted[r, pl.ds(start, count), :]
            return acc

        return lax.fori_loop(0, span // 8, tap_rows, jnp.zeros((count, LANES), F32))

    def forward(l, carry):
        lanes = lane(l)
        full = total + span
        streams = []
        for s in range(3):
            x = pext[s, :, lanes].astype(F32)
            st = short_ref[s, :, lanes]
            size = total if s == 0 else full
            low = halo + total - size
            acc = jnp.zeros((size, LANES), F32)
            for j in range(shorts):
                acc = acc + st[j : j + 1] * x[low - j : low - j + size]
            streams.append(acc.astype(BF16))
            if s == 0:
                query[:, lanes] = streams[0].astype(F32)
            else:
                bext[s, 0:total, lanes] = streams[s][span:]
        mixed = streams[1].astype(F32) * streams[2].astype(F32)
        for r in range(8):
            shifted[r, 8:full, :] = mixed[8 - r : full - r]
        half = total // 2
        for b in range(2):
            at = slice(b * half, (b + 1) * half)
            value = correlate(lanes, half, b * half + span, -1)
            inner[at, lanes] = value
            gated[at, lanes] = (query[at, lanes] * value).astype(BF16)
        return carry

    def grad_step(k):
        if k < n:
            step(grads, gg, k, grad_gate)

    lax.fori_loop(0, tiles // 2, forward, 0)
    grad_step(1)
    lax.fori_loop(tiles // 2, tiles, forward, 0)

    chunk = min(1024, width)

    def part_out(shard, d):
        at = pl.ds(pl.multiple_of(shard * rows, 16), rows)
        return jnp.dot(gated[at, :], o[:, d : d + chunk], preferred_element_type=F32)

    def part_act(shard, d):
        at = pl.ds(pl.multiple_of(shard * rows, 16), rows)
        value = None
        for s in range(3):
            term = lax.dot_general(
                gproj[s, at, :], w[s, d : d + chunk, :], NT, preferred_element_type=F32
            )
            value = term if value is None else value + term
        return value

    def fill(buf, part, shard):
        for d in range(0, width, chunk):
            buf[shard, :, d : d + chunk] = part(shard, d).astype(BF16)

    def add(buf, arrived, shard):
        for d in range(0, width, chunk):
            at = slice(d, d + chunk)
            buf[shard, :, at] = (
                buf[shard, :, at].astype(F32) + arrived[shard, :, at].astype(F32)
            ).astype(BF16)

    def r_copy(buf, land, s, shard, where):
        return to(buf.at[shard], land.at[shard], s[0].at[shard], s[1].at[shard], where)

    def l_copy(buf, land, s, shard, where):
        return to(buf.at[shard], land.at[shard], s[2].at[shard], s[3].at[shard], where)

    def reduce_step(t, buf, land_l, land_r, s, part):
        kr = t - me
        kl = t - (n - 1 - me)
        to_r, to_l = n - 1 - kr, kl
        go_r = (kr >= 0) & (to_r > me)
        go_l = (kl >= 0) & (to_l < me)

        @pl.when(go_r)
        def _():
            fill(buf, part, to_r)

            @pl.when(has_left)
            def _():
                r_copy(buf, land_l, s, to_r, left).wait_recv()
                add(buf, land_l, to_r)

            r_copy(buf, land_l, s, to_r, right).start()

        @pl.when(go_l)
        def _():
            fill(buf, part, to_l)

            @pl.when(has_right)
            def _():
                l_copy(buf, land_r, s, to_l, right).wait_recv()
                add(buf, land_r, to_l)

            l_copy(buf, land_r, s, to_l, left).start()

    def reduce_end(buf, land_l, land_r, s, part, result):
        for d in range(0, width, chunk):
            result[:, d : d + chunk] = part(me, d).astype(BF16)

        @pl.when(has_left)
        def _():
            r_copy(buf, land_l, s, me, left).wait_recv()

        @pl.when(has_right)
        def _():
            l_copy(buf, land_r, s, me, right).wait_recv()

        for cond, land in ((has_left, land_l), (has_right, land_r)):
            @pl.when(cond)
            def _(land=land):
                for d in range(0, width, chunk):
                    at = slice(d, d + chunk)
                    result[:, at] = (
                        result[:, at].astype(F32) + land[me, :, at].astype(F32)
                    ).astype(BF16)

        def one(i, carry):
            @pl.when(i > me)
            def _():
                r_copy(buf, land_l, s, i, right).wait_send()

            @pl.when(i < me)
            def _():
                l_copy(buf, land_r, s, i, left).wait_send()

            return carry

        lax.fori_loop(0, n, one, 0)

    out_args = (rs1, rs1_l, rs1_r, sems[8:12], part_out)
    act_args = (rs2, rs2_l, rs2_r, sems[12:16], part_act)

    grad_step(2)
    reduce_step(0, *out_args)
    for k in range(3, n):
        grad_step(k)

    def gate_back(l, carry):
        lanes = lane(l)
        g = ggate[:, lanes]
        gext[0:total, lanes] = (g * query[:, lanes]).astype(BF16)
        bext[0, 0:total, lanes] = (g * inner[:, lanes]).astype(BF16)
        return carry

    lax.fori_loop(0, tiles, gate_back, 0)

    def back_halo(where):
        return (
            to(gext.at[pl.ds(0, halo), :], gext.at[pl.ds(total, halo), :],
               halo_send.at[1], halo_recv.at[1], where),
            to(bext.at[:, pl.ds(0, 16), :], bext.at[:, pl.ds(total, 16), :],
               halo_send.at[2], halo_recv.at[2], where),
        )

    @pl.when(has_prev)
    def _():
        for copy in back_halo({"ctx": blk - 1, "tp": me}):
            copy.start()

    reduce_step(1, *out_args)

    @pl.when(has_next)
    def _():
        for copy in back_halo({"ctx": blk + 1, "tp": me}):
            copy.wait_recv()

    @pl.when(jnp.logical_not(has_next))
    def _():
        gext[total:, :] = jnp.zeros((halo, channels), BF16)
        bext[:, total:, :] = jnp.zeros((3, 16, channels), BF16)

    wide = total + 8

    def backward(l, carry):
        lanes = lane(l)
        x = gext[:, lanes].astype(F32)
        reach = total + halo - 8
        for r in range(8):
            shifted[r, 0:reach, :] = x[r : reach + r]
        count = wide // 3 if wide % 24 == 0 else wide
        mixed = jnp.concatenate(
            [correlate(lanes, count, b * count, 1) for b in range(wide // count)], axis=0
        )
        for s in range(3):
            other = bext[(0, 2, 1)[s], :, lanes].astype(F32)[0:wide]
            source = other if s == 0 else mixed * other
            st = short_ref[s, :, lanes]
            acc = jnp.zeros((total, LANES), F32)
            for j in range(shorts):
                acc = acc + st[j : j + 1] * source[j : j + total]
            gproj[s, :, lanes] = acc.astype(BF16)
        return carry

    lax.fori_loop(0, tiles // 2, backward, 0)
    for t in range(2, min(3, n - 1)):
        reduce_step(t, *out_args)
    lax.fori_loop(tiles // 2, tiles, backward, 0)
    for t in range(3, n - 1):
        reduce_step(t, *out_args)

    reduce_step(0, *act_args)
    reduce_end(*out_args, out_ref)
    for t in range(1, n - 1):
        reduce_step(t, *act_args)
    reduce_end(*act_args, dact_ref)

    gather_drain(acts, ga)
    gather_drain(grads, gg)

    @pl.when(has_next)
    def _():
        fwd_halo().wait_send()

    @pl.when(has_prev)
    def _():
        for copy in back_halo({"ctx": blk - 1, "tp": me}):
            copy.wait_send()


def body(activations, input_proj, short_taps, medium_taps, skip_gain, output_proj, out_grad):
    n = lax.axis_size("tp")
    blocks = lax.axis_size("ctx")
    rows, width = activations.shape
    channels = input_proj.shape[2]
    total = rows * n
    span = medium_taps.shape[1]
    lead = short_taps.shape[1] - 1
    halo = -(-(span + lead) // 16) * 16
    any_spec = pl.BlockSpec(memory_space=pl.ANY)
    vmem = pl.BlockSpec(memory_space=pltpu.VMEM)
    line = pltpu.VMEM((n, rows, width), BF16)
    dma = pltpu.SemaphoreType.DMA
    return pl.pallas_call(
        functools.partial(kernel, n, blocks, halo, lead),
        name="hyena",
        out_shape=(
            jax.ShapeDtypeStruct((rows, width), BF16),
            jax.ShapeDtypeStruct((rows, width), BF16),
        ),
        in_specs=[any_spec, any_spec, vmem, vmem, vmem, any_spec, any_spec],
        out_specs=(vmem, vmem),
        scratch_shapes=[
            pltpu.VMEM((3, width, channels), BF16),
            pltpu.VMEM((channels, width), BF16),
            line,
            line,
            pltpu.VMEM((span, channels), F32),
            pltpu.VMEM((3, halo + total, channels), BF16),
            pltpu.VMEM((3, total + 16, channels), BF16),
            pltpu.VMEM((total + halo, channels), BF16),
            pltpu.VMEM((total, channels), F32),
            pltpu.VMEM((total, channels), F32),
            pltpu.VMEM((total, channels), BF16),
            pltpu.VMEM((total, channels), F32),
            pltpu.VMEM((3, total, channels), BF16),
            pltpu.VMEM((8, total + halo, LANES), F32),
            line, line, line, line, line, line,
            dma((4,)),
            dma((1,)),
            dma((3,)),
            dma((3,)),
        ]
        + [dma((n,))] * 16,
        compiler_params=pltpu.CompilerParams(
            collective_id=0, has_side_effects=True, vmem_limit_bytes=60 * 1024 * 1024
        ),
    )(
        activations,
        jnp.transpose(input_proj, (1, 0, 2)),
        short_taps,
        medium_taps,
        skip_gain.reshape(1, channels),
        output_proj,
        out_grad,
    )


def solution(mesh):
    placed = (
        P(("ctx", "tp"), None),
        P(None, None, "tp"),
        P(None, None, "tp"),
        P("tp", None),
        P("tp"),
        P("tp", None),
        P(("ctx", "tp"), None),
    )
    return jax.shard_map(
        body,
        mesh=mesh,
        in_specs=placed,
        out_specs=(P(("ctx", "tp"), None), P(("ctx", "tp"), None)),
        check_vma=False,
    )
```

```python
import functools

import jax
import jax.numpy as jnp
from jax import lax
from jax.experimental import pallas as pl
from jax.experimental.pallas import tpu as pltpu
from jax.sharding import PartitionSpec as P

GROUP_SIZE = 16
LANES = 128
MESH = pl.DeviceIdType.MESH
F32 = jnp.float32
BF16 = jnp.bfloat16
NT = (((1,), (1,)), ((), ()))


def kernel(
    n, blocks, halo, lead,
    act_hbm, w_hbm, short_ref, med_ref, skip_ref, o_hbm, grad_hbm,
    out_ref, dact_ref,
    w, o, acts, grads, taps, pext, bext, gext, query, inner, gated, ggate, gproj, shifted,
    rs1, rs1_l, rs1_r, rs2, rs2_l, rs2_r,
    local_sem, bar_send, halo_send, halo_recv, *sems,
):
    me = lax.axis_index("tp")
    blk = lax.axis_index("ctx")
    rows, width = act_hbm.shape
    channels = w_hbm.shape[2]
    total = rows * n
    span = med_ref.shape[1]
    shorts = short_ref.shape[1]
    tiles = channels // LANES
    right = {"ctx": blk, "tp": me + 1}
    left = {"ctx": blk, "tp": me - 1}
    has_right = me + 1 < n
    has_left = me > 0
    has_next = blk + 1 < blocks
    has_prev = blk > 0

    def to(src, dst, send, recv, where):
        return pltpu.make_async_remote_copy(
            src_ref=src, dst_ref=dst, send_sem=send, recv_sem=recv,
            device_id=where, device_id_type=MESH,
        )

    loads = [
        pltpu.make_async_copy(act_hbm, acts.at[me], local_sem.at[0]),
        pltpu.make_async_copy(w_hbm, w, local_sem.at[1]),
        pltpu.make_async_copy(grad_hbm, grads.at[me], local_sem.at[2]),
        pltpu.make_async_copy(o_hbm, o, local_sem.at[3]),
    ]
    for load in loads:
        load.start()

    barrier = pltpu.get_barrier_semaphore()
    nbr = [
        (has_right, right), (has_left, left),
        (has_next, {"ctx": blk + 1, "tp": me}), (has_prev, {"ctx": blk - 1, "tp": me}),
    ]
    for cond, where in nbr:
        @pl.when(cond)
        def _(where=where):
            pl.semaphore_signal(barrier, inc=1, device_id=where, device_id_type=MESH)
    peers = sum(jnp.where(cond, 1, 0) for cond, _ in nbr)
    pl.semaphore_wait(barrier, peers)

    ga = sems[0:4]
    gg = sems[4:8]

    half = width // 2

    def cols(h):
        return pl.ds(pl.multiple_of(h * half, LANES), half)

    def piece(buf, s, shard, h, base, where, own=None):
        at = buf.at[shard, :, cols(h)]
        src = at if own is None else own.at[:, cols(h)]
        i = 2 * shard + h
        return to(src, at, s[base].at[i], s[base + 1].at[i], where)

    def send_own(buf, own, s, base, where):
        for h in range(2):
            piece(buf, s, me, h, base, where, own).start()

    def gather_drain(buf, s):
        def one(i, carry):
            for h in range(2):
                @pl.when(has_right & (i <= me))
                def _(h=h):
                    piece(buf, s, i, h, 0, right).wait_send()

                @pl.when(has_left & (i >= me))
                def _(h=h):
                    piece(buf, s, i, h, 2, left).wait_send()

            return carry

        lax.fori_loop(0, n, one, 0)

    def grad_own(step):
        @pl.when(has_right & (me == step))
        def _():
            send_own(grads, grad_hbm, gg, 0, right)

        @pl.when(has_left & (n - 1 - me == step))
        def _():
            send_own(grads, grad_hbm, gg, 2, left)

    @pl.when(has_right)
    def _():
        send_own(acts, act_hbm, ga, 0, right)

    @pl.when(has_left)
    def _():
        send_own(acts, act_hbm, ga, 2, left)

    grad_own(0)

    groups = med_ref.shape[0]
    ig = lax.broadcasted_iota(jnp.int32, (groups, channels), 0) * GROUP_SIZE
    ic = lax.broadcasted_iota(jnp.int32, (groups, channels), 1)
    spread = jnp.where((ic >= ig) & (ic < ig + GROUP_SIZE), 1.0, 0.0).astype(F32)
    taps[...] = lax.dot_general(
        med_ref[...], spread, (((0,), (0,)), ((), ())),
        precision=lax.Precision.HIGHEST, preferred_element_type=F32,
    )
    taps[0:1, :] = taps[0:1, :] + skip_ref[...]

    def project(shard):
        x = acts[shard]
        at = pl.ds(pl.multiple_of(halo + shard * rows, 16), rows)
        for s in range(3):
            pext[s, at, :] = jnp.dot(x, w[s], preferred_element_type=F32).astype(BF16)

    def grad_gate(shard):
        at = pl.ds(pl.multiple_of(shard * rows, 16), rows)
        ggate[at, :] = lax.dot_general(grads[shard], o[...], NT, preferred_element_type=F32)

    def pass_on(buf, s, k, h):
        l, r = me - k, me + k

        @pl.when(l >= 0)
        def _():
            piece(buf, s, l, h, 0, left).wait_recv()

            @pl.when(has_right)
            def _():
                piece(buf, s, l, h, 0, right).start()

        @pl.when(r < n)
        def _():
            piece(buf, s, r, h, 2, right).wait_recv()

            @pl.when(has_left)
            def _():
                piece(buf, s, r, h, 2, left).start()

    loads[0].wait()
    loads[1].wait()

    def act_step(i, carry):
        k, h = 1 + i // 2, i % 2

        @pl.when(i < 2 * (n - 1))
        def _():
            pass_on(acts, ga, k, h)

        @pl.when((h == 1) & (k < n))
        def _():
            grad_own(k)

        shard = jnp.where(h == 0, me + k - 1, me - k)

        @pl.when((shard >= 0) & (shard < n))
        def _():
            project(shard)

        return carry

    lax.fori_loop(0, 2 * n - 1, act_step, 0)

    def fwd_halo():
        return to(
            pext.at[:, pl.ds(total, halo), :], pext.at[:, pl.ds(0, halo), :],
            halo_send.at[0], halo_recv.at[0], {"ctx": blk + 1, "tp": me},
        )

    def fwd_halo_in():
        return to(
            pext.at[:, pl.ds(total, halo), :], pext.at[:, pl.ds(0, halo), :],
            halo_send.at[0], halo_recv.at[0], {"ctx": blk - 1, "tp": me},
        )

    @pl.when(has_next)
    def _():
        fwd_halo().start()

    loads[2].wait()
    loads[3].wait()
    grad_gate(me)

    @pl.when(has_prev)
    def _():
        fwd_halo_in().wait_recv()

    @pl.when(jnp.logical_not(has_prev))
    def _():
        pext[:, 0:halo, :] = jnp.zeros((3, halo, channels), BF16)

    def lane(l):
        return pl.ds(pl.multiple_of(l * LANES, LANES), LANES)

    def correlate(lanes, count, base, sign):
        def tap_rows(q, acc):
            block = taps[pl.ds(pl.multiple_of(8 * q, 8), 8), lanes]
            start = pl.multiple_of(base + sign * 8 * q, 8)
            for r in range(8):
                acc = acc + block[r : r + 1] * shifted[r, pl.ds(start, count), :]
            return acc

        return lax.fori_loop(0, span // 8, tap_rows, jnp.zeros((count, LANES), F32))

    def grad_step(i, carry):
        k, h = 1 + i // 2, i % 2

        @pl.when(k < n)
        def _():
            pass_on(grads, gg, k, h)

            @pl.when((h == 1) & (me - k >= 0))
            def _():
                grad_gate(me - k)

            @pl.when((h == 1) & (me + k < n))
            def _():
                grad_gate(me + k)

        return carry

    def forward(l, carry):
        lanes = lane(l)
        full = total + span
        streams = []
        for s in range(3):
            x = pext[s, :, lanes].astype(F32)
            st = short_ref[s, :, lanes]
            size = total if s == 0 else full
            low = halo + total - size
            acc = jnp.zeros((size, LANES), F32)
            for j in range(shorts):
                acc = acc + st[j : j + 1] * x[low - j : low - j + size]
            streams.append(acc.astype(BF16))
            if s == 0:
                query[:, lanes] = streams[0].astype(F32)
            else:
                bext[s, 0:total, lanes] = streams[s][span:]
        mixed = streams[1].astype(F32) * streams[2].astype(F32)
        for r in range(8):
            shifted[r, 8:full, :] = mixed[8 - r : full - r]
        count = total // 2
        for b in range(2):
            at = slice(b * count, (b + 1) * count)
            value = correlate(lanes, count, b * count + span, -1)
            inner[at, lanes] = value
            gated[at, lanes] = (query[at, lanes] * value).astype(BF16)
        return grad_step(l, carry)

    lax.fori_loop(0, tiles, forward, 0)

    chunk = min(1024, half)

    def part_out(shard, d):
        at = pl.ds(pl.multiple_of(shard * rows, 16), rows)
        return jnp.dot(gated[at, :], o[:, d : d + chunk], preferred_element_type=F32)

    def part_act(shard, d):
        at = pl.ds(pl.multiple_of(shard * rows, 16), rows)
        value = None
        for s in range(3):
            term = lax.dot_general(
                gproj[s, at, :], w[s, d : d + chunk, :], NT, preferred_element_type=F32
            )
            value = term if value is None else value + term
        return value

    def sum_copy(buf, land, s, shard, h, base, where):
        i = 2 * shard + h
        return to(
            buf.at[shard, :, cols(h)], land.at[shard, :, cols(h)],
            s[base].at[i], s[base + 1].at[i], where,
        )

    def hand_on(buf, land, s, part, shard, h, base, source, has_source, target):
        for d in range(h * half, (h + 1) * half, chunk):
            buf[shard, :, d : d + chunk] = part(shard, d).astype(BF16)

        @pl.when(has_source)
        def _():
            sum_copy(buf, land, s, shard, h, base, source).wait_recv()
            at = slice(h * half, (h + 1) * half)
            buf[shard, :, at] = (
                buf[shard, :, at].astype(F32) + land[shard, :, at].astype(F32)
            ).astype(BF16)

        sum_copy(buf, land, s, shard, h, base, target).start()

    def reduce_step(t, buf, land_l, land_r, s, part):
        kr = t - me
        kl = t - (n - 1 - me)
        to_r, to_l = n - 1 - kr, kl
        for h in range(2):
            @pl.when((kr >= 0) & (to_r > me))
            def _(h=h):
                hand_on(buf, land_l, s, part, to_r, h, 0, left, has_left, right)

            @pl.when((kl >= 0) & (to_l < me))
            def _(h=h):
                hand_on(buf, land_r, s, part, to_l, h, 2, right, has_right, left)

    def reduce_end(buf, land_l, land_r, s, part, result):
        for d in range(0, width, chunk):
            result[:, d : d + chunk] = part(me, d).astype(BF16)

        for h in range(2):
            for cond, land, base, source in (
                (has_left, land_l, 0, left), (has_right, land_r, 2, right)
            ):
                @pl.when(cond)
                def _(h=h, land=land, base=base, source=source):
                    sum_copy(buf, land, s, me, h, base, source).wait_recv()
                    at = slice(h * half, (h + 1) * half)
                    result[:, at] = (
                        result[:, at].astype(F32) + land[me, :, at].astype(F32)
                    ).astype(BF16)

        def one(i, carry):
            for h in range(2):
                @pl.when(i > me)
                def _(h=h):
                    sum_copy(buf, land_l, s, i, h, 0, right).wait_send()

                @pl.when(i < me)
                def _(h=h):
                    sum_copy(buf, land_r, s, i, h, 2, left).wait_send()

            return carry

        lax.fori_loop(0, n, one, 0)

    out_args = (rs1, rs1_l, rs1_r, sems[8:12], part_out)
    act_args = (rs2, rs2_l, rs2_r, sems[12:16], part_act)

    reduce_step(0, *out_args)
    lax.fori_loop(tiles, max(tiles, 2 * (n - 1)), grad_step, 0)

    def gate_back(l, carry):
        lanes = lane(l)
        g = ggate[:, lanes]
        gext[0:total, lanes] = (g * query[:, lanes]).astype(BF16)
        bext[0, 0:total, lanes] = (g * inner[:, lanes]).astype(BF16)
        return carry

    lax.fori_loop(0, tiles, gate_back, 0)

    def back_halo(where):
        return (
            to(gext.at[pl.ds(0, halo), :], gext.at[pl.ds(total, halo), :],
               halo_send.at[1], halo_recv.at[1], where),
            to(bext.at[:, pl.ds(0, 16), :], bext.at[:, pl.ds(total, 16), :],
               halo_send.at[2], halo_recv.at[2], where),
        )

    @pl.when(has_prev)
    def _():
        for copy in back_halo({"ctx": blk - 1, "tp": me}):
            copy.start()

    reduce_step(1, *out_args)

    @pl.when(has_next)
    def _():
        for copy in back_halo({"ctx": blk + 1, "tp": me}):
            copy.wait_recv()

    @pl.when(jnp.logical_not(has_next))
    def _():
        gext[total:, :] = jnp.zeros((halo, channels), BF16)
        bext[:, total:, :] = jnp.zeros((3, 16, channels), BF16)

    wide = total + 8

    def backward(l, carry):
        lanes = lane(l)
        x = gext[:, lanes].astype(F32)
        reach = total + halo - 8
        for r in range(8):
            shifted[r, 0:reach, :] = x[r : reach + r]
        count = wide // 3 if wide % 24 == 0 else wide
        mixed = jnp.concatenate(
            [correlate(lanes, count, b * count, 1) for b in range(wide // count)], axis=0
        )
        for s in range(3):
            other = bext[(0, 2, 1)[s], :, lanes].astype(F32)[0:wide]
            source = other if s == 0 else mixed * other
            st = short_ref[s, :, lanes]
            acc = jnp.zeros((total, LANES), F32)
            for j in range(shorts):
                acc = acc + st[j : j + 1] * source[j : j + total]
            gproj[s, :, lanes] = acc.astype(BF16)
        return carry

    lax.fori_loop(0, tiles // 2, backward, 0)
    for t in range(2, min(3, n - 1)):
        reduce_step(t, *out_args)
    lax.fori_loop(tiles // 2, tiles, backward, 0)
    for t in range(3, n - 1):
        reduce_step(t, *out_args)

    reduce_step(0, *act_args)
    reduce_end(*out_args, out_ref)
    for t in range(1, n - 1):
        reduce_step(t, *act_args)
    reduce_end(*act_args, dact_ref)

    gather_drain(acts, ga)
    gather_drain(grads, gg)

    @pl.when(has_next)
    def _():
        fwd_halo().wait_send()

    @pl.when(has_prev)
    def _():
        for copy in back_halo({"ctx": blk - 1, "tp": me}):
            copy.wait_send()


def body(activations, input_proj, short_taps, medium_taps, skip_gain, output_proj, out_grad):
    n = lax.axis_size("tp")
    blocks = lax.axis_size("ctx")
    rows, width = activations.shape
    channels = input_proj.shape[2]
    total = rows * n
    span = medium_taps.shape[1]
    lead = short_taps.shape[1] - 1
    halo = -(-(span + lead) // 16) * 16
    any_spec = pl.BlockSpec(memory_space=pl.ANY)
    vmem = pl.BlockSpec(memory_space=pltpu.VMEM)
    line = pltpu.VMEM((n, rows, width), BF16)
    dma = pltpu.SemaphoreType.DMA
    return pl.pallas_call(
        functools.partial(kernel, n, blocks, halo, lead),
        name="hyena",
        out_shape=(
            jax.ShapeDtypeStruct((rows, width), BF16),
            jax.ShapeDtypeStruct((rows, width), BF16),
        ),
        in_specs=[any_spec, any_spec, vmem, vmem, vmem, any_spec, any_spec],
        out_specs=(vmem, vmem),
        scratch_shapes=[
            pltpu.VMEM((3, width, channels), BF16),
            pltpu.VMEM((channels, width), BF16),
            line,
            line,
            pltpu.VMEM((span, channels), F32),
            pltpu.VMEM((3, halo + total, channels), BF16),
            pltpu.VMEM((3, total + 16, channels), BF16),
            pltpu.VMEM((total + halo, channels), BF16),
            pltpu.VMEM((total, channels), F32),
            pltpu.VMEM((total, channels), F32),
            pltpu.VMEM((total, channels), BF16),
            pltpu.VMEM((total, channels), F32),
            pltpu.VMEM((3, total, channels), BF16),
            pltpu.VMEM((8, total + halo, LANES), F32),
            line, line, line, line, line, line,
            dma((4,)),
            dma((1,)),
            dma((3,)),
            dma((3,)),
        ]
        + [dma((2 * n,))] * 16,
        compiler_params=pltpu.CompilerParams(
            collective_id=0, has_side_effects=True, vmem_limit_bytes=60 * 1024 * 1024
        ),
    )(
        activations,
        jnp.transpose(input_proj, (1, 0, 2)),
        short_taps,
        medium_taps,
        skip_gain.reshape(1, channels),
        output_proj,
        out_grad,
    )


def solution(mesh):
    placed = (
        P(("ctx", "tp"), None),
        P(None, None, "tp"),
        P(None, None, "tp"),
        P("tp", None),
        P("tp"),
        P("tp", None),
        P(("ctx", "tp"), None),
    )
    return jax.shard_map(
        body,
        mesh=mesh,
        in_specs=placed,
        out_specs=(P(("ctx", "tp"), None), P(("ctx", "tp"), None)),
        check_vma=False,
    )
```

```python
import functools

import jax
import jax.numpy as jnp
from jax import lax
from jax.experimental import pallas as pl
from jax.experimental.pallas import tpu as pltpu
from jax.sharding import PartitionSpec as P

GROUP_SIZE = 16
LANES = 128
MESH = pl.DeviceIdType.MESH
F32 = jnp.float32
BF16 = jnp.bfloat16
NT = (((1,), (1,)), ((), ()))


def kernel(
    n, blocks, halo, lead,
    act_hbm, w_hbm, short_ref, med_ref, skip_ref, o_hbm, grad_hbm,
    out_ref, dact_ref,
    w, o, acts, grads, taps, pext, bext, gext, query, inner, gated, ggate, gproj, shifted,
    rs1, rs1_l, rs1_r, rs2, rs2_l, rs2_r,
    local_sem, bar_send, halo_send, halo_recv, *sems,
):
    me = lax.axis_index("tp")
    blk = lax.axis_index("ctx")
    rows, width = act_hbm.shape
    channels = w_hbm.shape[2]
    total = rows * n
    span = med_ref.shape[1]
    shorts = short_ref.shape[1]
    tiles = channels // LANES
    right = {"ctx": blk, "tp": me + 1}
    left = {"ctx": blk, "tp": me - 1}
    has_right = me + 1 < n
    has_left = me > 0
    has_next = blk + 1 < blocks
    has_prev = blk > 0

    def to(src, dst, send, recv, where):
        return pltpu.make_async_remote_copy(
            src_ref=src, dst_ref=dst, send_sem=send, recv_sem=recv,
            device_id=where, device_id_type=MESH,
        )

    loads = [
        pltpu.make_async_copy(act_hbm, acts.at[me], local_sem.at[0]),
        pltpu.make_async_copy(w_hbm, w, local_sem.at[1]),
        pltpu.make_async_copy(grad_hbm, grads.at[me], local_sem.at[2]),
        pltpu.make_async_copy(o_hbm, o, local_sem.at[3]),
    ]
    for load in loads:
        load.start()

    barrier = pltpu.get_barrier_semaphore()
    nbr = [
        (has_right, right), (has_left, left),
        (has_next, {"ctx": blk + 1, "tp": me}), (has_prev, {"ctx": blk - 1, "tp": me}),
    ]
    for cond, where in nbr:
        @pl.when(cond)
        def _(where=where):
            pl.semaphore_signal(barrier, inc=1, device_id=where, device_id_type=MESH)
    peers = sum(jnp.where(cond, 1, 0) for cond, _ in nbr)
    pl.semaphore_wait(barrier, peers)

    ga = sems[0:4]
    gg = sems[4:8]

    half = width // 2

    def cols(h):
        return pl.ds(pl.multiple_of(h * half, LANES), half)

    def piece(buf, s, shard, h, base, where, own=None):
        at = buf.at[shard, :, cols(h)]
        src = at if own is None else own.at[:, cols(h)]
        i = 2 * shard + h
        return to(src, at, s[base].at[i], s[base + 1].at[i], where)

    def send_own(buf, own, s, base, where):
        for h in range(2):
            piece(buf, s, me, h, base, where, own).start()

    def gather_drain(buf, s):
        def one(i, carry):
            for h in range(2):
                @pl.when(has_right & (i <= me))
                def _(h=h):
                    piece(buf, s, i, h, 0, right).wait_send()

                @pl.when(has_left & (i >= me))
                def _(h=h):
                    piece(buf, s, i, h, 2, left).wait_send()

            return carry

        lax.fori_loop(0, n, one, 0)

    def grad_own(step):
        @pl.when(has_right & (me == step))
        def _():
            send_own(grads, grad_hbm, gg, 0, right)

        @pl.when(has_left & (n - 1 - me == step))
        def _():
            send_own(grads, grad_hbm, gg, 2, left)

    @pl.when(has_right)
    def _():
        send_own(acts, act_hbm, ga, 0, right)

    @pl.when(has_left)
    def _():
        send_own(acts, act_hbm, ga, 2, left)

    grad_own(0)

    groups = med_ref.shape[0]
    ig = lax.broadcasted_iota(jnp.int32, (groups, channels), 0) * GROUP_SIZE
    ic = lax.broadcasted_iota(jnp.int32, (groups, channels), 1)
    spread = jnp.where((ic >= ig) & (ic < ig + GROUP_SIZE), 1.0, 0.0).astype(F32)
    taps[...] = lax.dot_general(
        med_ref[...], spread, (((0,), (0,)), ((), ())),
        precision=lax.Precision.HIGHEST, preferred_element_type=F32,
    )
    taps[0:1, :] = taps[0:1, :] + skip_ref[...]

    def project(shard):
        x = acts[shard]
        at = pl.ds(pl.multiple_of(halo + shard * rows, 16), rows)
        for s in range(3):
            pext[s, at, :] = jnp.dot(x, w[s], preferred_element_type=F32).astype(BF16)

    def grad_gate(shard):
        at = pl.ds(pl.multiple_of(shard * rows, 16), rows)
        ggate[at, :] = lax.dot_general(grads[shard], o[...], NT, preferred_element_type=F32)

    def pass_on(buf, s, k, h):
        l, r = me - k, me + k

        @pl.when(l >= 0)
        def _():
            piece(buf, s, l, h, 0, left).wait_recv()

            @pl.when(has_right)
            def _():
                piece(buf, s, l, h, 0, right).start()

        @pl.when(r < n)
        def _():
            piece(buf, s, r, h, 2, right).wait_recv()

            @pl.when(has_left)
            def _():
                piece(buf, s, r, h, 2, left).start()

    loads[0].wait()
    loads[1].wait()

    def act_step(i, carry):
        k, h = 1 + i // 2, i % 2

        @pl.when(i < 2 * (n - 1))
        def _():
            pass_on(acts, ga, k, h)

        @pl.when((h == 1) & (k < n))
        def _():
            grad_own(k)

        shard = jnp.where(h == 0, me + k - 1, me - k)

        @pl.when((shard >= 0) & (shard < n))
        def _():
            project(shard)

        return carry

    lax.fori_loop(0, 2 * n - 1, act_step, 0)

    def fwd_halo():
        return to(
            pext.at[:, pl.ds(total, halo), :], pext.at[:, pl.ds(0, halo), :],
            halo_send.at[0], halo_recv.at[0], {"ctx": blk + 1, "tp": me},
        )

    def fwd_halo_in():
        return to(
            pext.at[:, pl.ds(total, halo), :], pext.at[:, pl.ds(0, halo), :],
            halo_send.at[0], halo_recv.at[0], {"ctx": blk - 1, "tp": me},
        )

    @pl.when(has_next)
    def _():
        fwd_halo().start()

    loads[2].wait()
    loads[3].wait()
    grad_gate(me)

    @pl.when(has_prev)
    def _():
        fwd_halo_in().wait_recv()

    @pl.when(jnp.logical_not(has_prev))
    def _():
        pext[:, 0:halo, :] = jnp.zeros((3, halo, channels), BF16)

    def lane(l):
        return pl.ds(pl.multiple_of(l * LANES, LANES), LANES)

    def correlate(lanes, count, base, sign):
        def tap_rows(q, acc):
            block = taps[pl.ds(pl.multiple_of(8 * q, 8), 8), lanes]
            start = pl.multiple_of(base + sign * 8 * q, 8)
            for r in range(8):
                acc = acc + block[r : r + 1] * shifted[r, pl.ds(start, count), :]
            return acc

        return lax.fori_loop(0, span // 8, tap_rows, jnp.zeros((count, LANES), F32))

    def grad_step(i, carry):
        k, h = 1 + i // 2, i % 2

        @pl.when(k < n)
        def _():
            pass_on(grads, gg, k, h)

            @pl.when((h == 1) & (me - k >= 0))
            def _():
                grad_gate(me - k)

            @pl.when((h == 1) & (me + k < n))
            def _():
                grad_gate(me + k)

        return carry

    def forward(l, carry):
        lanes = lane(l)
        full = total + span
        streams = []
        for s in range(3):
            x = pext[s, :, lanes].astype(F32)
            st = short_ref[s, :, lanes]
            size = total if s == 0 else full
            low = halo + total - size
            acc = jnp.zeros((size, LANES), F32)
            for j in range(shorts):
                acc = acc + st[j : j + 1] * x[low - j : low - j + size]
            streams.append(acc.astype(BF16))
            if s == 0:
                query[:, lanes] = streams[0].astype(F32)
            else:
                bext[s, 0:total, lanes] = streams[s][span:]
        mixed = streams[1].astype(F32) * streams[2].astype(F32)
        for r in range(8):
            shifted[r, 8:full, :] = mixed[8 - r : full - r]
        count = total // 2
        for b in range(2):
            at = slice(b * count, (b + 1) * count)
            value = correlate(lanes, count, b * count + span, -1)
            inner[at, lanes] = value
            gated[at, lanes] = (query[at, lanes] * value).astype(BF16)
        return grad_step(l, carry)

    lax.fori_loop(0, tiles, forward, 0)

    cuts = 4
    cut = width // cuts
    chunk = min(1024, cut)

    def part_out(shard, d):
        at = pl.ds(pl.multiple_of(shard * rows, 16), rows)
        return jnp.dot(gated[at, :], o[:, d : d + chunk], preferred_element_type=F32)

    def part_act(shard, d):
        at = pl.ds(pl.multiple_of(shard * rows, 16), rows)
        value = None
        for s in range(3):
            term = lax.dot_general(
                gproj[s, at, :], w[s, d : d + chunk, :], NT, preferred_element_type=F32
            )
            value = term if value is None else value + term
        return value

    def sum_copy(buf, land, s, shard, h, base, where):
        i = cuts * shard + h
        return to(
            buf.at[shard, :, pl.ds(h * cut, cut)], land.at[shard, :, pl.ds(h * cut, cut)],
            s[base].at[i], s[base + 1].at[i], where,
        )

    def hand_on(buf, land, s, part, shard, h, base, source, has_source, target):
        for d in range(h * cut, (h + 1) * cut, chunk):
            buf[shard, :, d : d + chunk] = part(shard, d).astype(BF16)

        @pl.when(has_source)
        def _():
            sum_copy(buf, land, s, shard, h, base, source).wait_recv()
            at = slice(h * cut, (h + 1) * cut)
            buf[shard, :, at] = (
                buf[shard, :, at].astype(F32) + land[shard, :, at].astype(F32)
            ).astype(BF16)

        sum_copy(buf, land, s, shard, h, base, target).start()

    def reduce_step(t, buf, land_l, land_r, s, part):
        kr = t - me
        kl = t - (n - 1 - me)
        to_r, to_l = n - 1 - kr, kl
        for h in range(cuts):
            @pl.when((kr >= 0) & (to_r > me))
            def _(h=h):
                hand_on(buf, land_l, s, part, to_r, h, 0, left, has_left, right)

            @pl.when((kl >= 0) & (to_l < me))
            def _(h=h):
                hand_on(buf, land_r, s, part, to_l, h, 2, right, has_right, left)

    def reduce_end(buf, land_l, land_r, s, part, result):
        for d in range(0, width, chunk):
            result[:, d : d + chunk] = part(me, d).astype(BF16)

        for h in range(cuts):
            for cond, land, base, source in (
                (has_left, land_l, 0, left), (has_right, land_r, 2, right)
            ):
                @pl.when(cond)
                def _(h=h, land=land, base=base, source=source):
                    sum_copy(buf, land, s, me, h, base, source).wait_recv()
                    at = slice(h * cut, (h + 1) * cut)
                    result[:, at] = (
                        result[:, at].astype(F32) + land[me, :, at].astype(F32)
                    ).astype(BF16)

        def one(i, carry):
            for h in range(cuts):
                @pl.when(i > me)
                def _(h=h):
                    sum_copy(buf, land_l, s, i, h, 0, right).wait_send()

                @pl.when(i < me)
                def _(h=h):
                    sum_copy(buf, land_r, s, i, h, 2, left).wait_send()

            return carry

        lax.fori_loop(0, n, one, 0)

    out_args = (rs1, rs1_l, rs1_r, sems[8:12], part_out)
    act_args = (rs2, rs2_l, rs2_r, sems[12:16], part_act)

    reduce_step(0, *out_args)
    lax.fori_loop(tiles, max(tiles, 2 * (n - 1)), grad_step, 0)

    def gate_back(l, carry):
        lanes = lane(l)
        g = ggate[:, lanes]
        gext[0:total, lanes] = (g * query[:, lanes]).astype(BF16)
        bext[0, 0:total, lanes] = (g * inner[:, lanes]).astype(BF16)
        return carry

    lax.fori_loop(0, tiles, gate_back, 0)

    def back_halo(where):
        return (
            to(gext.at[pl.ds(0, halo), :], gext.at[pl.ds(total, halo), :],
               halo_send.at[1], halo_recv.at[1], where),
            to(bext.at[:, pl.ds(0, 16), :], bext.at[:, pl.ds(total, 16), :],
               halo_send.at[2], halo_recv.at[2], where),
        )

    @pl.when(has_prev)
    def _():
        for copy in back_halo({"ctx": blk - 1, "tp": me}):
            copy.start()

    reduce_step(1, *out_args)

    @pl.when(has_next)
    def _():
        for copy in back_halo({"ctx": blk + 1, "tp": me}):
            copy.wait_recv()

    @pl.when(jnp.logical_not(has_next))
    def _():
        gext[total:, :] = jnp.zeros((halo, channels), BF16)
        bext[:, total:, :] = jnp.zeros((3, 16, channels), BF16)

    wide = total + 8

    def backward(l, carry):
        lanes = lane(l)
        x = gext[:, lanes].astype(F32)
        reach = total + halo - 8
        for r in range(8):
            shifted[r, 0:reach, :] = x[r : reach + r]
        count = wide // 3 if wide % 24 == 0 else wide
        mixed = jnp.concatenate(
            [correlate(lanes, count, b * count, 1) for b in range(wide // count)], axis=0
        )
        for s in range(3):
            other = bext[(0, 2, 1)[s], :, lanes].astype(F32)[0:wide]
            source = other if s == 0 else mixed * other
            st = short_ref[s, :, lanes]
            acc = jnp.zeros((total, LANES), F32)
            for j in range(shorts):
                acc = acc + st[j : j + 1] * source[j : j + total]
            gproj[s, :, lanes] = acc.astype(BF16)
        return carry

    lax.fori_loop(0, tiles // 2, backward, 0)
    for t in range(2, min(3, n - 1)):
        reduce_step(t, *out_args)
    lax.fori_loop(tiles // 2, tiles, backward, 0)
    for t in range(3, n - 1):
        reduce_step(t, *out_args)

    reduce_step(0, *act_args)
    reduce_end(*out_args, out_ref)
    for t in range(1, n - 1):
        reduce_step(t, *act_args)
    reduce_end(*act_args, dact_ref)

    gather_drain(acts, ga)
    gather_drain(grads, gg)

    @pl.when(has_next)
    def _():
        fwd_halo().wait_send()

    @pl.when(has_prev)
    def _():
        for copy in back_halo({"ctx": blk - 1, "tp": me}):
            copy.wait_send()


def body(activations, input_proj, short_taps, medium_taps, skip_gain, output_proj, out_grad):
    n = lax.axis_size("tp")
    blocks = lax.axis_size("ctx")
    rows, width = activations.shape
    channels = input_proj.shape[2]
    total = rows * n
    span = medium_taps.shape[1]
    lead = short_taps.shape[1] - 1
    halo = -(-(span + lead) // 16) * 16
    any_spec = pl.BlockSpec(memory_space=pl.ANY)
    vmem = pl.BlockSpec(memory_space=pltpu.VMEM)
    line = pltpu.VMEM((n, rows, width), BF16)
    dma = pltpu.SemaphoreType.DMA
    return pl.pallas_call(
        functools.partial(kernel, n, blocks, halo, lead),
        name="hyena",
        out_shape=(
            jax.ShapeDtypeStruct((rows, width), BF16),
            jax.ShapeDtypeStruct((rows, width), BF16),
        ),
        in_specs=[any_spec, any_spec, vmem, vmem, vmem, any_spec, any_spec],
        out_specs=(vmem, vmem),
        scratch_shapes=[
            pltpu.VMEM((3, width, channels), BF16),
            pltpu.VMEM((channels, width), BF16),
            line,
            line,
            pltpu.VMEM((span, channels), F32),
            pltpu.VMEM((3, halo + total, channels), BF16),
            pltpu.VMEM((3, total + 16, channels), BF16),
            pltpu.VMEM((total + halo, channels), BF16),
            pltpu.VMEM((total, channels), F32),
            pltpu.VMEM((total, channels), F32),
            pltpu.VMEM((total, channels), BF16),
            pltpu.VMEM((total, channels), F32),
            pltpu.VMEM((3, total, channels), BF16),
            pltpu.VMEM((8, total + halo, LANES), F32),
            line, line, line, line, line, line,
            dma((4,)),
            dma((1,)),
            dma((3,)),
            dma((3,)),
        ]
        + [dma((2 * n,))] * 8
        + [dma((4 * n,))] * 8,
        compiler_params=pltpu.CompilerParams(
            collective_id=0, has_side_effects=True, vmem_limit_bytes=60 * 1024 * 1024
        ),
    )(
        activations,
        jnp.transpose(input_proj, (1, 0, 2)),
        short_taps,
        medium_taps,
        skip_gain.reshape(1, channels),
        output_proj,
        out_grad,
    )


def solution(mesh):
    placed = (
        P(("ctx", "tp"), None),
        P(None, None, "tp"),
        P(None, None, "tp"),
        P("tp", None),
        P("tp"),
        P("tp", None),
        P(("ctx", "tp"), None),
    )
    return jax.shard_map(
        body,
        mesh=mesh,
        in_specs=placed,
        out_specs=(P(("ctx", "tp"), None), P(("ctx", "tp"), None)),
        check_vma=False,
    )
```
